32 devices in a mesh: rep: 2 (over x), shard: 4 (over y, core), ctx: 4 (over z).
Axes of the slice: x: 2, y: 2, z: 4, core: 2. Of those that a mesh axis runs over, the one named last changes fastest.
Arguments:
- tokens: bfloat16 [16, 256, 1024], P(('rep', 'shard'), 'ctx'), may hold values from -6 to 6
- positions: int32 [16, 256], P(('rep', 'shard')), may hold values from 0 to 255, as said below
- segments: int32 [16, 256], P(('rep', 'shard')), may hold values from 0 to 2, as said below
- cotangent: bfloat16 [16, 256, 1024], P(('rep', 'shard'), 'ctx'), may hold values from -6 to 6
- w_query: bfloat16 [1024, 2048], P(None, ('shard', 'ctx')), may hold values from -0.1875 to 0.1875
- key_weight: bfloat16 [1024, 1024], P(None, ('shard', 'ctx')), may hold values from -0.1875 to 0.1875
- value_weight: bfloat16 [1024, 1024], P(None, ('shard', 'ctx')), may hold values from -0.1875 to 0.1875
- output_weight: bfloat16 [2048, 1024], P(('shard', 'ctx')), may hold values from -0.625 to 0.625
- w_gate: bfloat16 [1024, 3072], P(None, ('shard', 'ctx')), may hold values from -0.1875 to 0.1875
- w_up: bfloat16 [1024, 3072], P(None, ('shard', 'ctx')), may hold values from -0.1875 to 0.1875
- w_down: bfloat16 [3072, 1024], P(('shard', 'ctx')), may hold values from -0.109375 to 0.109375
- norm_gains: bfloat16 [2304], P(('shard', 'ctx')), may hold values from 0.5 to 1.5
Outputs:
- block_out: bfloat16 [16, 256, 1024], P(('rep', 'shard'), 'ctx')
- grad_input: float32 [16, 256, 1024], P(('rep', 'shard'), 'ctx')
- grad_query: float32 [1024, 2048], P(None, ('shard', 'ctx'))
- grad_key: float32 [1024, 1024], P(None, ('shard', 'ctx'))
- grad_value: float32 [1024, 1024], P(None, ('shard', 'ctx'))
- grad_output: float32 [2048, 1024], P(('shard', 'ctx'))
- grad_gate: float32 [1024, 3072], P(None, ('shard', 'ctx'))
- grad_up: float32 [1024, 3072], P(None, ('shard', 'ctx'))
- grad_down: float32 [3072, 1024], P(('shard', 'ctx'))
- grad_gains: float32 [2304], P(('shard', 'ctx'))
The draws below stay inside these ranges and needn't reach their ends.
Inputs may be any that keep to these rules, and one draw needn't show every extreme that they name: In each sequence the stored positions are a permutation of all its positions made of runs of 32 consecutive positions; the two runs held by one index of ctx are the k-th from the start and the k-th from the end of the sequence, with k drawn per sequence. `segments`: ordered by position, a sequence's document numbers never fall, start at 0 and use every number up to 2.
All inputs are finite; a program needn't handle non-finite values.
Results may differ from the reference program's by a relative error of at most 0.02.
Values may be sent and summed in bfloat16 or wider, within the bound.
A program may use at most 192 MiB of HBM per device.

```python
import math
import jax
import jax.numpy as jnp
from jax import lax

MODEL_DIM = 1024
QUERY_HEADS = 16
KEY_VALUE_HEADS = 8
HEAD_DIM = 128
FF = 3072
SPAN = 32
DOCS = 3
SEQ_LEN = 256
BATCH = 16
GAINS = 2304


def layout_tables(key):
    pair_count = SEQ_LEN // (2 * SPAN)
    within = jnp.arange(SPAN, dtype=jnp.int32)

    def one_sequence(sub_key):
        order_key, cut_key = jax.random.split(sub_key)
        span_order = jax.random.permutation(order_key, pair_count).astype(jnp.int32)
        mirrored = 2 * pair_count - 1 - span_order
        span_ids = jnp.stack([span_order, mirrored], axis=1).reshape(2 * pair_count)
        stored = (span_ids[:, None] * SPAN + within[None, :]).reshape(SEQ_LEN)
        cut_all = jax.random.permutation(cut_key, SEQ_LEN - 1).astype(jnp.int32) + 1
        cut_points = cut_all[:DOCS - 1]
        doc_ids = jnp.sum((cut_points[None, :] <= stored[:, None]).astype(jnp.int32), axis=1)
        return (stored, doc_ids.astype(jnp.int32))
    seq_keys = jax.random.split(jax.random.fold_in(key, 7), BATCH)
    return jax.vmap(one_sequence)(seq_keys)


def draw_positions(key, part):
    return layout_tables(key)[0]


def draw_segments(key, part):
    return layout_tables(key)[1]


def level_of(rng, shape, shards, least, largest):
    level, own = 1.0, jax.random.fold_in(rng, 6)
    for axis_at, blocks in shards:
        heights = jnp.exp(jax.random.uniform(jax.random.fold_in(own, axis_at), (blocks,), jnp.float32, least / len(shards), largest / len(shards)))
        level = level * jnp.repeat(heights, shape[axis_at] // blocks).reshape([-1 if axis == axis_at else 1 for axis in range(len(shape))])
    return level


def centred(key, shape, width, limit, pieces=(), kind=jnp.bfloat16):
    array = jax.random.normal(key, shape, jnp.float32) * width
    if len(pieces) > 0:
        array = level_of(key, shape, pieces, -0.22, 0.18) * array
    return jnp.clip(array, min=-limit, max=limit).astype(kind)


def setup_inputs(seed: int = 0) -> dict:
    streams_of = jax.random.split(jax.random.key(seed), 13)
    return {
        "tokens": centred(streams_of[0], (BATCH, SEQ_LEN, MODEL_DIM), 1.0, 6.0, ((0, 8), (1, 4))),
        "positions": draw_positions(jax.random.fold_in(streams_of[12], 71), 0),
        "segments": draw_segments(jax.random.fold_in(streams_of[12], 71), 0),
        "cotangent": centred(streams_of[3], (BATCH, SEQ_LEN, MODEL_DIM), 1.0, 6.0, ((0, 8), (1, 4))),
        "w_query": centred(streams_of[4], (MODEL_DIM, QUERY_HEADS * HEAD_DIM), MODEL_DIM ** -0.5, 0.1875, ((1, 16),)),
        "key_weight": centred(streams_of[5], (MODEL_DIM, KEY_VALUE_HEADS * HEAD_DIM), MODEL_DIM ** -0.5, 0.1875, ((1, 16),)),
        "value_weight": centred(streams_of[6], (MODEL_DIM, KEY_VALUE_HEADS * HEAD_DIM), MODEL_DIM ** -0.5, 0.1875, ((1, 16),)),
        "output_weight": centred(streams_of[7], (QUERY_HEADS * HEAD_DIM, MODEL_DIM), (max(1, QUERY_HEADS * HEAD_DIM * 4 * DOCS // SEQ_LEN)) ** -0.5, 0.625, ((0, 16),)),
        "w_gate": centred(streams_of[8], (MODEL_DIM, FF), MODEL_DIM ** -0.5, 0.1875, ((1, 16),)),
        "w_up": centred(streams_of[9], (MODEL_DIM, FF), MODEL_DIM ** -0.5, 0.1875, ((1, 16),)),
        "w_down": centred(streams_of[10], (FF, MODEL_DIM), FF ** -0.5, 0.109375, ((0, 16),)),
        "norm_gains": jnp.clip(1.0 + 0.1 * jax.random.normal(streams_of[11], (GAINS,), jnp.float32), 0.5, 1.5).astype(jnp.bfloat16),
    }


EPSILON = 1e-06
ROPE_BASE = 1000000.0
HIGH = lax.Precision.HIGHEST

def rms_scale(values_in):
    return lax.rsqrt(lax.optimization_barrier(jnp.mean(values_in * values_in, axis=-1, keepdims=True)) + EPSILON)

def norm_backward(grad_in, values_in, scale_in, gain_in):
    grad_norm = grad_in * gain_in
    unit = values_in * scale_in
    return scale_in * (grad_norm - unit * lax.optimization_barrier(jnp.mean(grad_norm * unit, axis=-1, keepdims=True)))

def rope_tables(position_ids):
    half_dim = HEAD_DIM // 2
    inverse = 1.0 / ROPE_BASE ** (jnp.arange(half_dim, dtype=jnp.float32) * (2.0 / HEAD_DIM))
    angle = position_ids.astype(jnp.float32)[..., None] * inverse
    return (jnp.cos(angle)[:, :, None, :], jnp.sin(angle)[:, :, None, :])

def rotate(values_in, cosine, sine):
    half_dim = values_in.shape[-1] // 2
    first = values_in[..., :half_dim]
    second = values_in[..., half_dim:]
    return jnp.concatenate([first * cosine - second * sine, second * cosine + first * sine], axis=-1)

def rotate_back(grad_in, cosine, sine):
    half_dim = grad_in.shape[-1] // 2
    first = grad_in[..., :half_dim]
    second = grad_in[..., half_dim:]
    return jnp.concatenate([first * cosine + second * sine, second * cosine - first * sine], axis=-1)

def float_product(left, right):
    return jnp.dot(left, right, preferred_element_type=jnp.float32)

def layer_block(tokens, positions, segments, cotangent, weights):
    w_query, key_weight, value_weight, output_weight, w_gate, w_up, w_down, gain_all = weights
    sequence_count, sequence_length, model_width = tokens.shape
    total_rows = sequence_count * sequence_length
    group_width = QUERY_HEADS // KEY_VALUE_HEADS
    score_scale = 1.0 / math.sqrt(HEAD_DIM)
    g_attn = gain_all[:MODEL_DIM]
    g_query = gain_all[MODEL_DIM:MODEL_DIM + HEAD_DIM]
    key_gain = gain_all[MODEL_DIM + HEAD_DIM:MODEL_DIM + 2 * HEAD_DIM]
    g_mlp = gain_all[MODEL_DIM + 2 * HEAD_DIM:]
    x_rows = tokens.reshape(total_rows, MODEL_DIM).astype(jnp.float32)
    scale_in = rms_scale(x_rows)
    normed_input = (x_rows * scale_in * g_attn).astype(jnp.bfloat16)
    query = float_product(normed_input, w_query).reshape(sequence_count, sequence_length, QUERY_HEADS, HEAD_DIM)
    key_rows = float_product(normed_input, key_weight).reshape(sequence_count, sequence_length, KEY_VALUE_HEADS, HEAD_DIM)
    value_rows = float_product(normed_input, value_weight).astype(jnp.bfloat16).reshape(sequence_count, sequence_length, KEY_VALUE_HEADS, HEAD_DIM)
    q_scale = rms_scale(query)
    key_scale = rms_scale(key_rows)
    cosine, sine = rope_tables(positions)
    query_rotated = rotate(query * q_scale * g_query, cosine, sine).astype(jnp.bfloat16)
    k_rot = rotate(key_rows * key_scale * key_gain, cosine, sine).astype(jnp.bfloat16)
    allowed = ((segments[:, :, None] == segments[:, None, :]) & (positions[:, None, :] <= positions[:, :, None]))[:, None, None]
    query_group = query_rotated.reshape(sequence_count, sequence_length, KEY_VALUE_HEADS, group_width, HEAD_DIM).astype(jnp.float32)
    k_float = k_rot.astype(jnp.float32)
    v_float = value_rows.astype(jnp.float32)
    scores = jnp.einsum('bqkgd,bskd->bkgqs', query_group, k_float, precision=HIGH) * score_scale
    exponent = jnp.where(allowed, jnp.exp(scores), 0.0)
    denominator = lax.optimization_barrier(jnp.sum(exponent, axis=-1))
    log_total = jnp.log(denominator)
    probs = (exponent / denominator[..., None]).astype(jnp.bfloat16)
    attention_output = jnp.einsum('bkgqs,bskd->bqkgd', probs.astype(jnp.float32), v_float, precision=HIGH)
    attention_output = attention_output.astype(jnp.bfloat16).reshape(total_rows, QUERY_HEADS * HEAD_DIM)
    mixed_in = x_rows + float_product(attention_output, output_weight)
    scale_mid = rms_scale(mixed_in)
    normed_mid = (mixed_in * scale_mid * g_mlp).astype(jnp.bfloat16)
    gate_pre = float_product(normed_mid, w_gate)
    up_pre = float_product(normed_mid, w_up)
    sigmoid_gate = jax.nn.sigmoid(gate_pre)
    hidden = (gate_pre * sigmoid_gate * up_pre).astype(jnp.bfloat16)
    block_sum = mixed_in + float_product(hidden, w_down)
    block_out = block_sum.astype(jnp.bfloat16).reshape(sequence_count, sequence_length, MODEL_DIM)
    grad_rows = cotangent.reshape(total_rows, MODEL_DIM)
    d_hidden = float_product(grad_rows, w_down.T)
    grad_down = float_product(hidden.T, grad_rows)
    d_gate = (d_hidden * up_pre * sigmoid_gate * (1.0 + gate_pre * (1.0 - sigmoid_gate))).astype(jnp.bfloat16)
    d_up = (d_hidden * gate_pre * sigmoid_gate).astype(jnp.bfloat16)
    grad_gate = float_product(normed_mid.T, d_gate)
    grad_up = float_product(normed_mid.T, d_up)
    d_mid = float_product(d_gate, w_gate.T) + float_product(d_up, w_up.T)
    dg_mlp = lax.optimization_barrier(jnp.sum(d_mid * mixed_in * scale_mid, axis=0))
    d_resid = grad_rows.astype(jnp.float32) + norm_backward(d_mid, mixed_in, scale_mid, g_mlp)
    residual_gradient_bfloat = d_resid.astype(jnp.bfloat16)
    grad_output = float_product(attention_output.T, residual_gradient_bfloat)
    attention_gradient = float_product(residual_gradient_bfloat, output_weight.T).astype(jnp.bfloat16).reshape(sequence_count, sequence_length, KEY_VALUE_HEADS, group_width, HEAD_DIM)
    d_att_float = attention_gradient.astype(jnp.float32)
    attention_float = attention_output.reshape(sequence_count, sequence_length, KEY_VALUE_HEADS, group_width, HEAD_DIM).astype(jnp.float32)
    row_delta = jnp.transpose(lax.optimization_barrier(jnp.sum(d_att_float * attention_float, axis=-1)), (0, 2, 3, 1))
    probs_back = jnp.where(allowed, jnp.exp(scores - log_total[..., None]), 0.0)
    probs_round = probs_back.astype(jnp.bfloat16).astype(jnp.float32)
    values_gradient = jnp.einsum('bkgqs,bqkgd->bskd', probs_round, d_att_float, precision=HIGH)
    d_probs = jnp.einsum('bqkgd,bskd->bkgqs', d_att_float, v_float, precision=HIGH)
    d_scores = (probs_back * (d_probs - row_delta[..., None])).astype(jnp.bfloat16).astype(jnp.float32)
    d_qrot = jnp.einsum('bkgqs,bskd->bqkgd', d_scores, k_float, precision=HIGH) * score_scale
    d_krot = jnp.einsum('bkgqs,bqkgd->bskd', d_scores, query_group, precision=HIGH) * score_scale
    d_qn = rotate_back(d_qrot.reshape(sequence_count, sequence_length, QUERY_HEADS, HEAD_DIM), cosine, sine)
    normed_key_gradient = rotate_back(d_krot, cosine, sine)
    dg_query = lax.optimization_barrier(jnp.sum(d_qn * query * q_scale, axis=(0, 1, 2)))
    dg_key = lax.optimization_barrier(jnp.sum(normed_key_gradient * key_rows * key_scale, axis=(0, 1, 2)))
    d_query = norm_backward(d_qn, query, q_scale, g_query).astype(jnp.bfloat16).reshape(total_rows, QUERY_HEADS * HEAD_DIM)
    key_gradient = norm_backward(normed_key_gradient, key_rows, key_scale, key_gain).astype(jnp.bfloat16).reshape(total_rows, KEY_VALUE_HEADS * HEAD_DIM)
    value_gradient = values_gradient.astype(jnp.bfloat16).reshape(total_rows, KEY_VALUE_HEADS * HEAD_DIM)
    grad_query = float_product(normed_input.T, d_query)
    grad_key = float_product(normed_input.T, key_gradient)
    grad_value = float_product(normed_input.T, value_gradient)
    d_in = float_product(d_query, w_query.T) + float_product(key_gradient, key_weight.T) + float_product(value_gradient, value_weight.T)
    dg_attn = lax.optimization_barrier(jnp.sum(d_in * x_rows * scale_in, axis=0))
    grad_input = (d_resid + norm_backward(d_in, x_rows, scale_in, g_attn)).reshape(sequence_count, sequence_length, MODEL_DIM)
    grad_gains = jnp.concatenate([dg_attn, dg_query, dg_key, dg_mlp])
    grads = (grad_query, grad_key, grad_value, grad_output, grad_gate, grad_up, grad_down, grad_gains)
    return (block_out, grad_input, grads)

def reference(tokens, positions, segments, cotangent, w_query, key_weight, value_weight, output_weight, w_gate, w_up, w_down, norm_gains):
    group_count = math.gcd(BATCH, max(1, 4096 // SEQ_LEN))
    step_count = BATCH // group_count
    weights = (w_query, key_weight, value_weight, output_weight, w_gate, w_up, w_down, norm_gains.astype(jnp.float32))

    def split_groups(array_in):
        return array_in.reshape((step_count, group_count) + array_in.shape[1:])
    initial = tuple((jnp.zeros(wt.shape, jnp.float32) for wt in weights[:7])) + (jnp.zeros((GAINS,), jnp.float32),)

    def advance(carry, item):
        block_out, grad_input, grads = layer_block(item[0], item[1], item[2], item[3], weights)
        return (tuple((c_old + g_new for c_old, g_new in zip(carry, grads))), (block_out, grad_input))
    carry, stacked = lax.scan(advance, initial, (split_groups(tokens), split_groups(positions), split_groups(segments), split_groups(cotangent)))
    block_out = stacked[0].reshape(BATCH, SEQ_LEN, MODEL_DIM)
    grad_input = stacked[1].reshape(BATCH, SEQ_LEN, MODEL_DIM)
    return (block_out, grad_input, carry[0], carry[1], carry[2], carry[3], carry[4], carry[5], carry[6], carry[7])
```

```python
import math

import jax
import jax.numpy as jnp
from jax import lax
from jax.sharding import PartitionSpec as P

QUERY_HEADS = 16
KEY_VALUE_HEADS = 8
HEAD_DIM = 128


EPSILON = 1e-06
ROPE_BASE = 1000000.0


def rms_scale(values_in):
    return lax.rsqrt(jnp.mean(values_in * values_in, axis=-1, keepdims=True) + EPSILON)


def norm_backward(grad_in, values_in, scale_in, gain_in):
    grad_norm = grad_in * gain_in
    unit = values_in * scale_in
    return scale_in * (grad_norm - unit * jnp.mean(grad_norm * unit, axis=-1, keepdims=True))


def rope_tables(position_ids):
    half_dim = HEAD_DIM // 2
    inverse = 1.0 / ROPE_BASE ** (jnp.arange(half_dim, dtype=jnp.float32) * (2.0 / HEAD_DIM))
    angle = position_ids.astype(jnp.float32)[..., None] * inverse
    return (jnp.cos(angle)[:, :, None, :], jnp.sin(angle)[:, :, None, :])


def rotate(values_in, cosine, sine):
    half_dim = values_in.shape[-1] // 2
    first = values_in[..., :half_dim]
    second = values_in[..., half_dim:]
    return jnp.concatenate(
        [first * cosine - second * sine, second * cosine + first * sine], axis=-1
    )


def rotate_back(grad_in, cosine, sine):
    half_dim = grad_in.shape[-1] // 2
    first = grad_in[..., :half_dim]
    second = grad_in[..., half_dim:]
    return jnp.concatenate(
        [first * cosine + second * sine, second * cosine - first * sine], axis=-1
    )


def float_product(left, right):
    return jnp.dot(left, right, preferred_element_type=jnp.float32)


def against_rows(left, right):
    return lax.dot_general(
        left, right, (((1,), (1,)), ((), ())), preferred_element_type=jnp.float32
    )


def over_tokens(left, right):
    return lax.dot_general(
        left, right, (((0,), (0,)), ((), ())), preferred_element_type=jnp.float32
    )


def body(
    tokens,
    positions,
    segments,
    cotangent,
    w_query,
    key_weight,
    value_weight,
    output_weight,
    w_gate,
    w_up,
    w_down,
    norm_gains,
):
    sequence_count, local_length, model_width = tokens.shape
    total_rows = sequence_count * local_length
    group_width = QUERY_HEADS // KEY_VALUE_HEADS
    score_scale = 1.0 / math.sqrt(HEAD_DIM)
    local_start = lax.axis_index("ctx") * local_length
    local_pos = lax.dynamic_slice_in_dim(positions, local_start, local_length, 1)
    local_seg = lax.dynamic_slice_in_dim(segments, local_start, local_length, 1)
    wq_full, full_key_weight, full_value_weight, wo_full, gains_full = (
        lax.all_gather(w_query, ("shard", "ctx"), axis=1, tiled=True),
        lax.all_gather(key_weight, ("shard", "ctx"), axis=1, tiled=True),
        lax.all_gather(value_weight, ("shard", "ctx"), axis=1, tiled=True),
        lax.all_gather(output_weight, ("shard", "ctx"), axis=0, tiled=True),
        lax.all_gather(norm_gains, ("shard", "ctx"), axis=0, tiled=True),
    )
    gain_all = gains_full.astype(jnp.float32)
    g_attn = gain_all[:model_width]
    g_query = gain_all[model_width : model_width + HEAD_DIM]
    key_gain = gain_all[model_width + HEAD_DIM : model_width + 2 * HEAD_DIM]
    g_mlp = gain_all[model_width + 2 * HEAD_DIM :]
    x_rows = tokens.reshape(total_rows, model_width).astype(jnp.float32)
    scale_in = rms_scale(x_rows)
    normed_input = (x_rows * scale_in * g_attn).astype(jnp.bfloat16)
    query = float_product(normed_input, wq_full).reshape(
        sequence_count, local_length, QUERY_HEADS, HEAD_DIM
    )
    key_rows = float_product(normed_input, full_key_weight).reshape(
        sequence_count, local_length, KEY_VALUE_HEADS, HEAD_DIM
    )
    value_rows = (
        float_product(normed_input, full_value_weight)
        .astype(jnp.bfloat16)
        .reshape(sequence_count, local_length, KEY_VALUE_HEADS, HEAD_DIM)
    )
    q_scale = rms_scale(query)
    key_scale = rms_scale(key_rows)
    cosine, sine = rope_tables(local_pos)
    query_rotated = rotate(query * q_scale * g_query, cosine, sine).astype(jnp.bfloat16)
    k_rot = rotate(key_rows * key_scale * key_gain, cosine, sine).astype(jnp.bfloat16)
    keys_all, values_all = (
        lax.all_gather(k_rot, "ctx", axis=1, tiled=True),
        lax.all_gather(value_rows, "ctx", axis=1, tiled=True),
    )
    allowed = (
        (local_seg[:, :, None] == segments[:, None, :])
        & (positions[:, None, :] <= local_pos[:, :, None])
    )[:, None, None]
    query_group = query_rotated.reshape(
        sequence_count, local_length, KEY_VALUE_HEADS, group_width, HEAD_DIM
    )
    scores = (
        jnp.einsum("bqkgd,bskd->bkgqs", query_group, keys_all, preferred_element_type=jnp.float32)
        * score_scale
    )
    exponent = jnp.where(allowed, jnp.exp(scores), 0.0)
    denominator = jnp.sum(exponent, axis=-1)
    log_total = jnp.log(denominator)
    probs = (exponent / denominator[..., None]).astype(jnp.bfloat16)
    attention_output = jnp.einsum(
        "bkgqs,bskd->bqkgd", probs, values_all, preferred_element_type=jnp.float32
    )
    attention_output = attention_output.astype(jnp.bfloat16).reshape(
        total_rows, QUERY_HEADS * HEAD_DIM
    )
    mixed_in = x_rows + float_product(attention_output, wo_full)
    scale_mid = rms_scale(mixed_in)
    normed_mid = (mixed_in * scale_mid * g_mlp).astype(jnp.bfloat16)
    wg_full, wu_full, wd_full = (
        lax.all_gather(w_gate, ("shard", "ctx"), axis=1, tiled=True),
        lax.all_gather(w_up, ("shard", "ctx"), axis=1, tiled=True),
        lax.all_gather(w_down, ("shard", "ctx"), axis=0, tiled=True),
    )
    gate_pre = float_product(normed_mid, wg_full)
    up_pre = float_product(normed_mid, wu_full)
    sigmoid_gate = jax.nn.sigmoid(gate_pre)
    hidden = (gate_pre * sigmoid_gate * up_pre).astype(jnp.bfloat16)
    block_sum = mixed_in + float_product(hidden, wd_full)
    block_out = block_sum.astype(jnp.bfloat16).reshape(sequence_count, local_length, model_width)
    grad_rows = cotangent.reshape(total_rows, model_width)
    d_hidden = against_rows(grad_rows, wd_full)
    grad_down = over_tokens(hidden, grad_rows)
    d_gate = (d_hidden * up_pre * sigmoid_gate * (1.0 + gate_pre * (1.0 - sigmoid_gate))).astype(
        jnp.bfloat16
    )
    d_up = (d_hidden * gate_pre * sigmoid_gate).astype(jnp.bfloat16)
    grad_gate = over_tokens(normed_mid, d_gate)
    grad_up = over_tokens(normed_mid, d_up)
    owned_gate, owned_up, owned_down = (
        lax.psum_scatter(grad_gate, ("shard", "ctx"), scatter_dimension=1, tiled=True),
        lax.psum_scatter(grad_up, ("shard", "ctx"), scatter_dimension=1, tiled=True),
        lax.psum_scatter(grad_down, ("shard", "ctx"), scatter_dimension=0, tiled=True),
    )
    total_gate, total_up, total_down = (
        lax.psum(owned_gate.astype(jnp.bfloat16), "rep").astype(jnp.float32),
        lax.psum(owned_up.astype(jnp.bfloat16), "rep").astype(jnp.float32),
        lax.psum(owned_down.astype(jnp.bfloat16), "rep").astype(jnp.float32),
    )
    d_mid = against_rows(d_gate, wg_full) + against_rows(d_up, wu_full)
    dg_mlp = jnp.sum(d_mid * mixed_in * scale_mid, axis=0)
    d_resid = grad_rows.astype(jnp.float32) + norm_backward(d_mid, mixed_in, scale_mid, g_mlp)
    residual_gradient_bfloat = d_resid.astype(jnp.bfloat16)
    grad_output = over_tokens(attention_output, residual_gradient_bfloat)
    attention_gradient = (
        against_rows(residual_gradient_bfloat, wo_full)
        .astype(jnp.bfloat16)
        .reshape(sequence_count, local_length, KEY_VALUE_HEADS, group_width, HEAD_DIM)
    )
    attention_heads = attention_output.reshape(
        sequence_count, local_length, KEY_VALUE_HEADS, group_width, HEAD_DIM
    )
    row_delta = jnp.sum(
        attention_gradient.astype(jnp.float32) * attention_heads.astype(jnp.float32), axis=-1
    )
    row_delta = jnp.transpose(row_delta, (0, 2, 3, 1))
    scores_again = (
        jnp.einsum("bqkgd,bskd->bkgqs", query_group, keys_all, preferred_element_type=jnp.float32)
        * score_scale
    )
    probs_back = jnp.where(allowed, jnp.exp(scores_again - log_total[..., None]), 0.0)
    probs_round = probs_back.astype(jnp.bfloat16)
    values_gradient = jnp.einsum(
        "bkgqs,bqkgd->bskd", probs_round, attention_gradient, preferred_element_type=jnp.float32
    )
    d_probs = jnp.einsum(
        "bqkgd,bskd->bkgqs", attention_gradient, values_all, preferred_element_type=jnp.float32
    )
    d_scores = (probs_back * (d_probs - row_delta[..., None])).astype(jnp.bfloat16)
    d_qrot = (
        jnp.einsum("bkgqs,bskd->bqkgd", d_scores, keys_all, preferred_element_type=jnp.float32)
        * score_scale
    )
    d_krot = (
        jnp.einsum("bkgqs,bqkgd->bskd", d_scores, query_group, preferred_element_type=jnp.float32)
        * score_scale
    )
    d_keys, value_rows_gradient = (
        lax.psum_scatter(
            d_krot.astype(jnp.bfloat16), "ctx", scatter_dimension=1, tiled=True
        ).astype(jnp.float32),
        lax.psum_scatter(
            values_gradient.astype(jnp.bfloat16), "ctx", scatter_dimension=1, tiled=True
        ).astype(jnp.float32),
    )
    d_qn = rotate_back(
        d_qrot.reshape(sequence_count, local_length, QUERY_HEADS, HEAD_DIM), cosine, sine
    )
    normed_key_gradient = rotate_back(d_keys, cosine, sine)
    dg_query = jnp.sum(d_qn * query * q_scale, axis=(0, 1, 2))
    dg_key = jnp.sum(normed_key_gradient * key_rows * key_scale, axis=(0, 1, 2))
    d_query = (
        norm_backward(d_qn, query, q_scale, g_query)
        .astype(jnp.bfloat16)
        .reshape(total_rows, QUERY_HEADS * HEAD_DIM)
    )
    key_gradient = (
        norm_backward(normed_key_gradient, key_rows, key_scale, key_gain)
        .astype(jnp.bfloat16)
        .reshape(total_rows, KEY_VALUE_HEADS * HEAD_DIM)
    )
    value_gradient = value_rows_gradient.astype(jnp.bfloat16).reshape(
        total_rows, KEY_VALUE_HEADS * HEAD_DIM
    )
    grad_query = over_tokens(normed_input, d_query)
    grad_key = over_tokens(normed_input, key_gradient)
    grad_value = over_tokens(normed_input, value_gradient)
    d_in = (
        against_rows(d_query, wq_full)
        + against_rows(key_gradient, full_key_weight)
        + against_rows(value_gradient, full_value_weight)
    )
    dg_attn = jnp.sum(d_in * x_rows * scale_in, axis=0)
    grad_input = (d_resid + norm_backward(d_in, x_rows, scale_in, g_attn)).reshape(
        sequence_count, local_length, model_width
    )
    grad_gains = jnp.concatenate([dg_attn, dg_query, dg_key, dg_mlp])
    owned_query, owned_key, owned_value, owned_output, owned_gains = (
        lax.psum_scatter(grad_query, ("shard", "ctx"), scatter_dimension=1, tiled=True),
        lax.psum_scatter(grad_key, ("shard", "ctx"), scatter_dimension=1, tiled=True),
        lax.psum_scatter(grad_value, ("shard", "ctx"), scatter_dimension=1, tiled=True),
        lax.psum_scatter(grad_output, ("shard", "ctx"), scatter_dimension=0, tiled=True),
        lax.psum_scatter(grad_gains, ("shard", "ctx"), scatter_dimension=0, tiled=True),
    )
    total_query, total_key, total_value, total_output, total_gains = (
        lax.psum(owned_query.astype(jnp.bfloat16), "rep").astype(jnp.float32),
        lax.psum(owned_key.astype(jnp.bfloat16), "rep").astype(jnp.float32),
        lax.psum(owned_value.astype(jnp.bfloat16), "rep").astype(jnp.float32),
        lax.psum(owned_output.astype(jnp.bfloat16), "rep").astype(jnp.float32),
        lax.psum(owned_gains.astype(jnp.bfloat16), "rep").astype(jnp.float32),
    )
    return (
        block_out,
        grad_input,
        total_query,
        total_key,
        total_value,
        total_output,
        total_gate,
        total_up,
        total_down,
        total_gains,
    )


def gather_ctx(rows_in):
    return lax.all_gather(rows_in, "ctx", axis=1, tiled=True)


def scatter_ctx(partial, sequence_count):
    total_rows, width = partial.shape
    shaped = partial.astype(jnp.bfloat16).reshape(sequence_count, total_rows // sequence_count, width)
    owned = lax.psum_scatter(shaped, "ctx", scatter_dimension=1, tiled=True)
    return owned.astype(jnp.float32).reshape(-1, width)


def gather_columns(block):
    gathered = lax.all_gather(block, "shard", axis=0, tiled=False)
    return jnp.transpose(gathered, (1, 0, 2))


def finish(owned):
    return lax.psum(owned.astype(jnp.bfloat16), "rep").astype(jnp.float32)


def head_parallel_body(
    tokens,
    positions,
    segments,
    cotangent,
    w_query,
    key_weight,
    value_weight,
    output_weight,
    w_gate,
    w_up,
    w_down,
    norm_gains,
):
    sequence_count, local_length, model_width = tokens.shape
    context_size = lax.axis_size("ctx")
    shard_size = lax.axis_size("shard")
    full_length = local_length * context_size
    half_width = key_weight.shape[1]
    ff_width = w_gate.shape[1]
    heads = shard_size
    score_scale = 1.0 / math.sqrt(HEAD_DIM)
    odd = lax.rem(lax.axis_index("ctx"), 2) == 1
    partners = [(i, i + 1 - 2 * (i % 2)) for i in range(context_size)]

    own_kv = jnp.concatenate([key_weight, value_weight], axis=1)
    peer_kv = lax.ppermute(own_kv, "ctx", partners)
    low = jnp.where(odd, peer_kv, own_kv)
    high = jnp.where(odd, own_kv, peer_kv)
    qkv_block = jnp.concatenate(
        [
            w_query,
            low[:, :half_width],
            high[:, :half_width],
            low[:, half_width:],
            high[:, half_width:],
        ],
        axis=1,
    )
    x_all = gather_ctx(tokens)
    gain_all = lax.all_gather(norm_gains, ("shard", "ctx"), axis=0, tiled=True).astype(jnp.float32)
    qkv_full = gather_columns(qkv_block)
    wo_full = lax.all_gather(output_weight, "shard", axis=0, tiled=True)
    gu_full = gather_columns(jnp.concatenate([w_gate, w_up], axis=1)).reshape(model_width, -1)
    wd_full = lax.all_gather(w_down, "shard", axis=0, tiled=True)
    grad_all = gather_ctx(cotangent).reshape(-1, model_width)

    wq_full = qkv_full[:, :, :HEAD_DIM].reshape(model_width, -1)
    wk_full = qkv_full[:, :, HEAD_DIM : 2 * HEAD_DIM].reshape(model_width, -1)
    wv_full = qkv_full[:, :, 2 * HEAD_DIM :].reshape(model_width, -1)
    g_attn = gain_all[:model_width]
    g_query = gain_all[model_width : model_width + HEAD_DIM]
    key_gain = gain_all[model_width + HEAD_DIM : model_width + 2 * HEAD_DIM]
    g_mlp = gain_all[model_width + 2 * HEAD_DIM :]

    x_full = x_all.reshape(-1, model_width).astype(jnp.float32)
    normed_input = (x_full * rms_scale(x_full) * g_attn).astype(jnp.bfloat16)
    head_shape = (sequence_count, full_length, heads, HEAD_DIM)
    query = float_product(normed_input, wq_full).reshape(head_shape)
    key_rows = float_product(normed_input, wk_full).reshape(head_shape)
    value_rows = float_product(normed_input, wv_full).astype(jnp.bfloat16).reshape(head_shape)
    q_scale = rms_scale(query)
    key_scale = rms_scale(key_rows)
    cosine, sine = rope_tables(positions)
    q_rot = rotate(query * q_scale * g_query, cosine, sine).astype(jnp.bfloat16)
    k_rot = rotate(key_rows * key_scale * key_gain, cosine, sine).astype(jnp.bfloat16)
    allowed = (
        (segments[:, :, None] == segments[:, None, :])
        & (positions[:, None, :] <= positions[:, :, None])
    )[:, None]
    scores = (
        jnp.einsum("bqhd,bshd->bhqs", q_rot, k_rot, preferred_element_type=jnp.float32)
        * score_scale
    )
    exponent = jnp.where(allowed, jnp.exp(scores), 0.0)
    denominator = jnp.sum(exponent, axis=-1, keepdims=True)
    probs = exponent / denominator
    probs_round = probs.astype(jnp.bfloat16)
    attended = (
        jnp.einsum("bhqs,bshd->bqhd", probs_round, value_rows, preferred_element_type=jnp.float32)
        .astype(jnp.bfloat16)
    )
    attended_rows = attended.reshape(-1, heads * HEAD_DIM)
    x_rows = tokens.reshape(-1, model_width).astype(jnp.float32)
    mixed_in = x_rows + scatter_ctx(float_product(attended_rows, wo_full), sequence_count)
    scale_mid = rms_scale(mixed_in)
    local_shape = tokens.shape
    normed_mid = gather_ctx(
        (mixed_in * scale_mid * g_mlp).astype(jnp.bfloat16).reshape(local_shape)
    ).reshape(-1, model_width)

    d_hidden = against_rows(grad_all, wd_full)
    gate_up = float_product(normed_mid, gu_full).reshape(-1, shard_size, 2 * ff_width)
    gate_pre = gate_up[:, :, :ff_width].reshape(-1, shard_size * ff_width)
    up_pre = gate_up[:, :, ff_width:].reshape(-1, shard_size * ff_width)
    sigmoid_gate = jax.nn.sigmoid(gate_pre)
    hidden = (gate_pre * sigmoid_gate * up_pre).astype(jnp.bfloat16)
    d_gate = (d_hidden * up_pre * sigmoid_gate * (1.0 + gate_pre * (1.0 - sigmoid_gate))).astype(
        jnp.bfloat16
    )
    d_up = (d_hidden * gate_pre * sigmoid_gate).astype(jnp.bfloat16)
    d_gu = jnp.concatenate(
        [
            d_gate.reshape(-1, shard_size, ff_width),
            d_up.reshape(-1, shard_size, ff_width),
        ],
        axis=2,
    ).reshape(-1, 2 * shard_size * ff_width)
    d_mid = scatter_ctx(against_rows(d_gu, gu_full), sequence_count)
    grad_rows = cotangent.reshape(-1, model_width)
    dg_mlp = jnp.sum(d_mid * mixed_in * scale_mid, axis=0)
    d_resid = grad_rows.astype(jnp.float32) + norm_backward(d_mid, mixed_in, scale_mid, g_mlp)
    resid_all = gather_ctx(d_resid.astype(jnp.bfloat16).reshape(local_shape)).reshape(
        -1, model_width
    )

    block_sum = mixed_in + scatter_ctx(float_product(hidden, wd_full), sequence_count)
    block_out = block_sum.astype(jnp.bfloat16).reshape(local_shape)
    grad_gu = over_tokens(normed_mid, d_gu).astype(jnp.bfloat16)
    grad_gu = grad_gu.reshape(model_width, shard_size, 2 * ff_width)
    owned_gu = lax.psum_scatter(
        jnp.transpose(grad_gu, (1, 0, 2)), "shard", scatter_dimension=0, tiled=False
    )
    grad_down = over_tokens(hidden, grad_all).astype(jnp.bfloat16)
    owned_down = lax.psum_scatter(grad_down, "shard", scatter_dimension=0, tiled=True)
    total_gu, total_down = finish(owned_gu), finish(owned_down)

    d_att = against_rows(resid_all, wo_full).astype(jnp.bfloat16).reshape(head_shape)
    grad_output = over_tokens(attended_rows, resid_all).astype(jnp.bfloat16)
    row_delta = jnp.sum(d_att.astype(jnp.float32) * attended.astype(jnp.float32), axis=-1)
    row_delta = jnp.transpose(row_delta, (0, 2, 1))[..., None]
    d_values = jnp.einsum("bhqs,bqhd->bshd", probs_round, d_att, preferred_element_type=jnp.float32)
    d_probs = jnp.einsum("bqhd,bshd->bhqs", d_att, value_rows, preferred_element_type=jnp.float32)
    d_scores = (probs * (d_probs - row_delta)).astype(jnp.bfloat16)
    d_qrot = (
        jnp.einsum("bhqs,bshd->bqhd", d_scores, k_rot, preferred_element_type=jnp.float32)
        * score_scale
    )
    d_krot = (
        jnp.einsum("bhqs,bqhd->bshd", d_scores, q_rot, preferred_element_type=jnp.float32)
        * score_scale
    )
    d_qn = rotate_back(d_qrot, cosine, sine)
    d_kn = rotate_back(d_krot, cosine, sine)
    dg_query = jnp.sum(d_qn * query * q_scale, axis=(0, 1, 2))
    dg_key = jnp.sum(d_kn * key_rows * key_scale, axis=(0, 1, 2))
    d_query = norm_backward(d_qn, query, q_scale, g_query).astype(jnp.bfloat16)
    d_query = d_query.reshape(-1, heads * HEAD_DIM)
    d_key = norm_backward(d_kn, key_rows, key_scale, key_gain)
    d_key_b = d_key.astype(jnp.bfloat16)
    d_value_b = d_values.astype(jnp.bfloat16)
    d_in_part = (
        against_rows(d_query, wq_full)
        + against_rows(d_key_b.reshape(-1, heads * HEAD_DIM), wk_full)
        + against_rows(d_value_b.reshape(-1, heads * HEAD_DIM), wv_full)
    )
    kv_low = jnp.concatenate([d_key_b[..., :half_width], d_value_b[..., :half_width]], axis=-1)
    kv_high = jnp.concatenate([d_key_b[..., half_width:], d_value_b[..., half_width:]], axis=-1)
    kv_own = jnp.where(odd, kv_high, kv_low)
    kv_other = lax.ppermute(jnp.where(odd, kv_low, kv_high), "ctx", partners)
    kv_rows = (kv_own.astype(jnp.float32) + kv_other.astype(jnp.float32)).astype(jnp.bfloat16)
    kv_rows = kv_rows.reshape(-1, heads * 2 * half_width)
    d_in = scatter_ctx(d_in_part, sequence_count)
    grad_query = over_tokens(normed_input, d_query).astype(jnp.bfloat16)
    grad_kv = over_tokens(normed_input, kv_rows).astype(jnp.bfloat16)
    grad_qkv = jnp.concatenate(
        [
            grad_query.reshape(model_width, shard_size, HEAD_DIM),
            grad_kv.reshape(model_width, shard_size, 2 * half_width),
        ],
        axis=2,
    )
    owned_output = lax.psum_scatter(grad_output, "shard", scatter_dimension=0, tiled=True)
    owned_qkv = lax.psum_scatter(
        jnp.transpose(grad_qkv, (1, 0, 2)), "shard", scatter_dimension=0, tiled=False
    )
    total_output, total_qkv = finish(owned_output), finish(owned_qkv)
    scale_in = rms_scale(x_rows)
    dg_attn = jnp.sum(d_in * x_rows * scale_in, axis=0)
    grad_input = (d_resid + norm_backward(d_in, x_rows, scale_in, g_attn)).reshape(local_shape)
    grad_gains = jnp.concatenate([dg_attn, dg_query, dg_key, dg_mlp])
    owned_gains = lax.psum_scatter(
        grad_gains, ("shard", "ctx"), scatter_dimension=0, tiled=True
    )
    total_gains = finish(owned_gains)
    return (
        block_out,
        grad_input,
        total_qkv[:, :HEAD_DIM],
        total_qkv[:, HEAD_DIM : HEAD_DIM + half_width],
        total_qkv[:, HEAD_DIM + half_width :],
        total_output,
        total_gu[:, :ff_width],
        total_gu[:, ff_width:],
        total_down,
        total_gains,
    )


def any_body(*arguments):
    w_query, key_weight = arguments[4:6]
    whole_query_head = w_query.shape[1] == HEAD_DIM
    half_key_head = 2 * key_weight.shape[1] == HEAD_DIM
    if whole_query_head and half_key_head and lax.axis_size("ctx") % 2 == 0:
        return head_parallel_body(*arguments)
    return body(*arguments)


def solution(mesh):
    in_specs = (
        P(("rep", "shard"), "ctx", None),
        P(("rep", "shard"), None),
        P(("rep", "shard"), None),
        P(("rep", "shard"), "ctx", None),
        P(None, ("shard", "ctx")),
        P(None, ("shard", "ctx")),
        P(None, ("shard", "ctx")),
        P(("shard", "ctx"), None),
        P(None, ("shard", "ctx")),
        P(None, ("shard", "ctx")),
        P(("shard", "ctx"), None),
        P(("shard", "ctx")),
    )
    out_specs = (
        P(("rep", "shard"), "ctx", None),
        P(("rep", "shard"), "ctx", None),
        P(None, ("shard", "ctx")),
        P(None, ("shard", "ctx")),
        P(None, ("shard", "ctx")),
        P(("shard", "ctx"), None),
        P(None, ("shard", "ctx")),
        P(None, ("shard", "ctx")),
        P(("shard", "ctx"), None),
        P(("shard", "ctx")),
    )
    return jax.shard_map(any_body, mesh=mesh, in_specs=in_specs, out_specs=out_specs, check_vma=False)
```

```python
import math

import jax
import jax.numpy as jnp
from jax import lax
from jax.sharding import PartitionSpec as P

QUERY_HEADS = 16
KEY_VALUE_HEADS = 8
HEAD_DIM = 128


EPSILON = 1e-06
ROPE_BASE = 1000000.0


def rms_scale(values_in):
    return lax.rsqrt(jnp.mean(values_in * values_in, axis=-1, keepdims=True) + EPSILON)


def norm_backward(grad_in, values_in, scale_in, gain_in):
    grad_norm = grad_in * gain_in
    unit = values_in * scale_in
    return scale_in * (grad_norm - unit * jnp.mean(grad_norm * unit, axis=-1, keepdims=True))


def rope_tables(position_ids):
    half_dim = HEAD_DIM // 2
    inverse = 1.0 / ROPE_BASE ** (jnp.arange(half_dim, dtype=jnp.float32) * (2.0 / HEAD_DIM))
    angle = position_ids.astype(jnp.float32)[..., None] * inverse
    return (jnp.cos(angle)[:, :, None, :], jnp.sin(angle)[:, :, None, :])


def rotate(values_in, cosine, sine):
    half_dim = values_in.shape[-1] // 2
    first = values_in[..., :half_dim]
    second = values_in[..., half_dim:]
    return jnp.concatenate(
        [first * cosine - second * sine, second * cosine + first * sine], axis=-1
    )


def rotate_back(grad_in, cosine, sine):
    half_dim = grad_in.shape[-1] // 2
    first = grad_in[..., :half_dim]
    second = grad_in[..., half_dim:]
    return jnp.concatenate(
        [first * cosine + second * sine, second * cosine - first * sine], axis=-1
    )


def float_product(left, right):
    return jnp.dot(left, right, preferred_element_type=jnp.float32)


def against_rows(left, right):
    return lax.dot_general(
        left, right, (((1,), (1,)), ((), ())), preferred_element_type=jnp.float32
    )


def over_tokens(left, right):
    return lax.dot_general(
        left, right, (((0,), (0,)), ((), ())), preferred_element_type=jnp.float32
    )


def body(
    tokens,
    positions,
    segments,
    cotangent,
    w_query,
    key_weight,
    value_weight,
    output_weight,
    w_gate,
    w_up,
    w_down,
    norm_gains,
):
    sequence_count, local_length, model_width = tokens.shape
    total_rows = sequence_count * local_length
    group_width = QUERY_HEADS // KEY_VALUE_HEADS
    score_scale = 1.0 / math.sqrt(HEAD_DIM)
    local_start = lax.axis_index("ctx") * local_length
    local_pos = lax.dynamic_slice_in_dim(positions, local_start, local_length, 1)
    local_seg = lax.dynamic_slice_in_dim(segments, local_start, local_length, 1)
    wq_full, full_key_weight, full_value_weight, wo_full, gains_full = (
        lax.all_gather(w_query, ("shard", "ctx"), axis=1, tiled=True),
        lax.all_gather(key_weight, ("shard", "ctx"), axis=1, tiled=True),
        lax.all_gather(value_weight, ("shard", "ctx"), axis=1, tiled=True),
        lax.all_gather(output_weight, ("shard", "ctx"), axis=0, tiled=True),
        lax.all_gather(norm_gains, ("shard", "ctx"), axis=0, tiled=True),
    )
    gain_all = gains_full.astype(jnp.float32)
    g_attn = gain_all[:model_width]
    g_query = gain_all[model_width : model_width + HEAD_DIM]
    key_gain = gain_all[model_width + HEAD_DIM : model_width + 2 * HEAD_DIM]
    g_mlp = gain_all[model_width + 2 * HEAD_DIM :]
    x_rows = tokens.reshape(total_rows, model_width).astype(jnp.float32)
    scale_in = rms_scale(x_rows)
    normed_input = (x_rows * scale_in * g_attn).astype(jnp.bfloat16)
    query = float_product(normed_input, wq_full).reshape(
        sequence_count, local_length, QUERY_HEADS, HEAD_DIM
    )
    key_rows = float_product(normed_input, full_key_weight).reshape(
        sequence_count, local_length, KEY_VALUE_HEADS, HEAD_DIM
    )
    value_rows = (
        float_product(normed_input, full_value_weight)
        .astype(jnp.bfloat16)
        .reshape(sequence_count, local_length, KEY_VALUE_HEADS, HEAD_DIM)
    )
    q_scale = rms_scale(query)
    key_scale = rms_scale(key_rows)
    cosine, sine = rope_tables(local_pos)
    query_rotated = rotate(query * q_scale * g_query, cosine, sine).astype(jnp.bfloat16)
    k_rot = rotate(key_rows * key_scale * key_gain, cosine, sine).astype(jnp.bfloat16)
    keys_all, values_all = (
        lax.all_gather(k_rot, "ctx", axis=1, tiled=True),
        lax.all_gather(value_rows, "ctx", axis=1, tiled=True),
    )
    allowed = (
        (local_seg[:, :, None] == segments[:, None, :])
        & (positions[:, None, :] <= local_pos[:, :, None])
    )[:, None, None]
    query_group = query_rotated.reshape(
        sequence_count, local_length, KEY_VALUE_HEADS, group_width, HEAD_DIM
    )
    scores = (
        jnp.einsum("bqkgd,bskd->bkgqs", query_group, keys_all, preferred_element_type=jnp.float32)
        * score_scale
    )
    exponent = jnp.where(allowed, jnp.exp(scores), 0.0)
    denominator = jnp.sum(exponent, axis=-1)
    log_total = jnp.log(denominator)
    probs = (exponent / denominator[..., None]).astype(jnp.bfloat16)
    attention_output = jnp.einsum(
        "bkgqs,bskd->bqkgd", probs, values_all, preferred_element_type=jnp.float32
    )
    attention_output = attention_output.astype(jnp.bfloat16).reshape(
        total_rows, QUERY_HEADS * HEAD_DIM
    )
    mixed_in = x_rows + float_product(attention_output, wo_full)
    scale_mid = rms_scale(mixed_in)
    normed_mid = (mixed_in * scale_mid * g_mlp).astype(jnp.bfloat16)
    wg_full, wu_full, wd_full = (
        lax.all_gather(w_gate, ("shard", "ctx"), axis=1, tiled=True),
        lax.all_gather(w_up, ("shard", "ctx"), axis=1, tiled=True),
        lax.all_gather(w_down, ("shard", "ctx"), axis=0, tiled=True),
    )
    gate_pre = float_product(normed_mid, wg_full)
    up_pre = float_product(normed_mid, wu_full)
    sigmoid_gate = jax.nn.sigmoid(gate_pre)
    hidden = (gate_pre * sigmoid_gate * up_pre).astype(jnp.bfloat16)
    block_sum = mixed_in + float_product(hidden, wd_full)
    block_out = block_sum.astype(jnp.bfloat16).reshape(sequence_count, local_length, model_width)
    grad_rows = cotangent.reshape(total_rows, model_width)
    d_hidden = against_rows(grad_rows, wd_full)
    grad_down = over_tokens(hidden, grad_rows)
    d_gate = (d_hidden * up_pre * sigmoid_gate * (1.0 + gate_pre * (1.0 - sigmoid_gate))).astype(
        jnp.bfloat16
    )
    d_up = (d_hidden * gate_pre * sigmoid_gate).astype(jnp.bfloat16)
    grad_gate = over_tokens(normed_mid, d_gate)
    grad_up = over_tokens(normed_mid, d_up)
    owned_gate, owned_up, owned_down = (
        lax.psum_scatter(grad_gate, ("shard", "ctx"), scatter_dimension=1, tiled=True),
        lax.psum_scatter(grad_up, ("shard", "ctx"), scatter_dimension=1, tiled=True),
        lax.psum_scatter(grad_down, ("shard", "ctx"), scatter_dimension=0, tiled=True),
    )
    total_gate, total_up, total_down = (
        lax.psum(owned_gate.astype(jnp.bfloat16), "rep").astype(jnp.float32),
        lax.psum(owned_up.astype(jnp.bfloat16), "rep").astype(jnp.float32),
        lax.psum(owned_down.astype(jnp.bfloat16), "rep").astype(jnp.float32),
    )
    d_mid = against_rows(d_gate, wg_full) + against_rows(d_up, wu_full)
    dg_mlp = jnp.sum(d_mid * mixed_in * scale_mid, axis=0)
    d_resid = grad_rows.astype(jnp.float32) + norm_backward(d_mid, mixed_in, scale_mid, g_mlp)
    residual_gradient_bfloat = d_resid.astype(jnp.bfloat16)
    grad_output = over_tokens(attention_output, residual_gradient_bfloat)
    attention_gradient = (
        against_rows(residual_gradient_bfloat, wo_full)
        .astype(jnp.bfloat16)
        .reshape(sequence_count, local_length, KEY_VALUE_HEADS, group_width, HEAD_DIM)
    )
    attention_heads = attention_output.reshape(
        sequence_count, local_length, KEY_VALUE_HEADS, group_width, HEAD_DIM
    )
    row_delta = jnp.sum(
        attention_gradient.astype(jnp.float32) * attention_heads.astype(jnp.float32), axis=-1
    )
    row_delta = jnp.transpose(row_delta, (0, 2, 3, 1))
    scores_again = (
        jnp.einsum("bqkgd,bskd->bkgqs", query_group, keys_all, preferred_element_type=jnp.float32)
        * score_scale
    )
    probs_back = jnp.where(allowed, jnp.exp(scores_again - log_total[..., None]), 0.0)
    probs_round = probs_back.astype(jnp.bfloat16)
    values_gradient = jnp.einsum(
        "bkgqs,bqkgd->bskd", probs_round, attention_gradient, preferred_element_type=jnp.float32
    )
    d_probs = jnp.einsum(
        "bqkgd,bskd->bkgqs", attention_gradient, values_all, preferred_element_type=jnp.float32
    )
    d_scores = (probs_back * (d_probs - row_delta[..., None])).astype(jnp.bfloat16)
    d_qrot = (
        jnp.einsum("bkgqs,bskd->bqkgd", d_scores, keys_all, preferred_element_type=jnp.float32)
        * score_scale
    )
    d_krot = (
        jnp.einsum("bkgqs,bqkgd->bskd", d_scores, query_group, preferred_element_type=jnp.float32)
        * score_scale
    )
    d_keys, value_rows_gradient = (
        lax.psum_scatter(
            d_krot.astype(jnp.bfloat16), "ctx", scatter_dimension=1, tiled=True
        ).astype(jnp.float32),
        lax.psum_scatter(
            values_gradient.astype(jnp.bfloat16), "ctx", scatter_dimension=1, tiled=True
        ).astype(jnp.float32),
    )
    d_qn = rotate_back(
        d_qrot.reshape(sequence_count, local_length, QUERY_HEADS, HEAD_DIM), cosine, sine
    )
    normed_key_gradient = rotate_back(d_keys, cosine, sine)
    dg_query = jnp.sum(d_qn * query * q_scale, axis=(0, 1, 2))
    dg_key = jnp.sum(normed_key_gradient * key_rows * key_scale, axis=(0, 1, 2))
    d_query = (
        norm_backward(d_qn, query, q_scale, g_query)
        .astype(jnp.bfloat16)
        .reshape(total_rows, QUERY_HEADS * HEAD_DIM)
    )
    key_gradient = (
        norm_backward(normed_key_gradient, key_rows, key_scale, key_gain)
        .astype(jnp.bfloat16)
        .reshape(total_rows, KEY_VALUE_HEADS * HEAD_DIM)
    )
    value_gradient = value_rows_gradient.astype(jnp.bfloat16).reshape(
        total_rows, KEY_VALUE_HEADS * HEAD_DIM
    )
    grad_query = over_tokens(normed_input, d_query)
    grad_key = over_tokens(normed_input, key_gradient)
    grad_value = over_tokens(normed_input, value_gradient)
    d_in = (
        against_rows(d_query, wq_full)
        + against_rows(key_gradient, full_key_weight)
        + against_rows(value_gradient, full_value_weight)
    )
    dg_attn = jnp.sum(d_in * x_rows * scale_in, axis=0)
    grad_input = (d_resid + norm_backward(d_in, x_rows, scale_in, g_attn)).reshape(
        sequence_count, local_length, model_width
    )
    grad_gains = jnp.concatenate([dg_attn, dg_query, dg_key, dg_mlp])
    owned_query, owned_key, owned_value, owned_output, owned_gains = (
        lax.psum_scatter(grad_query, ("shard", "ctx"), scatter_dimension=1, tiled=True),
        lax.psum_scatter(grad_key, ("shard", "ctx"), scatter_dimension=1, tiled=True),
        lax.psum_scatter(grad_value, ("shard", "ctx"), scatter_dimension=1, tiled=True),
        lax.psum_scatter(grad_output, ("shard", "ctx"), scatter_dimension=0, tiled=True),
        lax.psum_scatter(grad_gains, ("shard", "ctx"), scatter_dimension=0, tiled=True),
    )
    total_query, total_key, total_value, total_output, total_gains = (
        lax.psum(owned_query.astype(jnp.bfloat16), "rep").astype(jnp.float32),
        lax.psum(owned_key.astype(jnp.bfloat16), "rep").astype(jnp.float32),
        lax.psum(owned_value.astype(jnp.bfloat16), "rep").astype(jnp.float32),
        lax.psum(owned_output.astype(jnp.bfloat16), "rep").astype(jnp.float32),
        lax.psum(owned_gains.astype(jnp.bfloat16), "rep").astype(jnp.float32),
    )
    return (
        block_out,
        grad_input,
        total_query,
        total_key,
        total_value,
        total_output,
        total_gate,
        total_up,
        total_down,
        total_gains,
    )


def shifted(block, offset):
    size = lax.axis_size("ctx")
    return lax.ppermute(block, "ctx", [(i, (i + offset) % size) for i in range(size)])


def gather_ctx(rows_in):
    size = lax.axis_size("ctx")
    return jnp.concatenate([rows_in] + [shifted(rows_in, k) for k in range(1, size)], axis=1)


def scatter_ctx(partial, sequence_count):
    size = lax.axis_size("ctx")
    total_rows, width = partial.shape
    shaped = partial.reshape(sequence_count, size, -1, width)
    owned = shaped[:, 0]
    for k in range(1, size):
        arrived = shifted(shaped[:, k].astype(jnp.bfloat16), -k)
        owned = owned + arrived.astype(jnp.float32)
    return owned.reshape(-1, width)


def slot_order(table, axis):
    size = lax.axis_size("ctx")
    length = table.shape[axis] // size
    here = lax.axis_index("ctx")
    return [
        lax.dynamic_slice_in_dim(table, lax.rem(here - k + size, size) * length, length, axis)
        for k in range(size)
    ]


def gather_columns(block):
    gathered = lax.all_gather(block, "shard", axis=0, tiled=False)
    return jnp.transpose(gathered, (1, 0, 2))


def finish(owned):
    part = owned.astype(jnp.bfloat16)
    if lax.axis_size("rep") != 2:
        return lax.psum(part, "rep").astype(jnp.float32)
    other = lax.ppermute(part, "rep", [(0, 1), (1, 0)])
    return part.astype(jnp.float32) + other.astype(jnp.float32)


def head_parallel_body(
    tokens,
    positions,
    segments,
    cotangent,
    w_query,
    key_weight,
    value_weight,
    output_weight,
    w_gate,
    w_up,
    w_down,
    norm_gains,
):
    sequence_count, local_length, model_width = tokens.shape
    context_size = lax.axis_size("ctx")
    shard_size = lax.axis_size("shard")
    full_length = local_length * context_size
    half_width = key_weight.shape[1]
    ff_width = w_gate.shape[1]
    heads = shard_size
    score_scale = 1.0 / math.sqrt(HEAD_DIM)
    odd = lax.rem(lax.axis_index("ctx"), 2) == 1
    partners = [(i, i + 1 - 2 * (i % 2)) for i in range(context_size)]

    own_kv = jnp.concatenate([key_weight, value_weight], axis=1)
    peer_kv = lax.ppermute(own_kv, "ctx", partners)
    low = jnp.where(odd, peer_kv, own_kv)
    high = jnp.where(odd, own_kv, peer_kv)
    qkv_block = jnp.concatenate(
        [
            w_query,
            low[:, :half_width],
            high[:, :half_width],
            low[:, half_width:],
            high[:, half_width:],
        ],
        axis=1,
    )
    x_all = gather_ctx(tokens)
    gain_count = norm_gains.shape[0]
    gain_slots = gather_ctx(norm_gains.reshape(1, gain_count)).reshape(-1)
    gain_order = jnp.concatenate(slot_order(gain_slots, 0))
    gain_rows = -(-gain_order.shape[0] // (8 * qkv_block.shape[1])) * 8
    gain_block = jnp.pad(
        gain_order, (0, gain_rows * qkv_block.shape[1] - gain_order.shape[0])
    ).reshape(gain_rows, -1)
    gathered = lax.all_gather(
        jnp.concatenate([qkv_block, gain_block], axis=0), "shard", axis=0, tiled=False
    )
    qkv_full = jnp.transpose(gathered[:, :model_width], (1, 0, 2))
    gain_all = (
        gathered[:, model_width:]
        .reshape(shard_size, -1)[:, : context_size * gain_count]
        .reshape(-1)
        .astype(jnp.float32)
    )
    wo_full = lax.all_gather(output_weight, "shard", axis=0, tiled=True)
    gu_full = gather_columns(jnp.concatenate([w_gate, w_up], axis=1)).reshape(model_width, -1)
    wd_full = lax.all_gather(w_down, "shard", axis=0, tiled=True)
    grad_all = gather_ctx(cotangent).reshape(-1, model_width)

    wq_full = qkv_full[:, :, :HEAD_DIM].reshape(model_width, -1)
    wk_full = qkv_full[:, :, HEAD_DIM : 2 * HEAD_DIM].reshape(model_width, -1)
    wv_full = qkv_full[:, :, 2 * HEAD_DIM :].reshape(model_width, -1)
    g_attn = gain_all[:model_width]
    g_query = gain_all[model_width : model_width + HEAD_DIM]
    key_gain = gain_all[model_width + HEAD_DIM : model_width + 2 * HEAD_DIM]
    g_mlp = gain_all[model_width + 2 * HEAD_DIM :]

    positions = jnp.concatenate(slot_order(positions, 1), axis=1)
    segments = jnp.concatenate(slot_order(segments, 1), axis=1)
    x_full = x_all.reshape(-1, model_width).astype(jnp.float32)
    scale_full = rms_scale(x_full)
    normed_input = (x_full * scale_full * g_attn).astype(jnp.bfloat16)
    head_shape = (sequence_count, full_length, heads, HEAD_DIM)
    query = float_product(normed_input, wq_full).reshape(head_shape)
    key_rows = float_product(normed_input, wk_full).reshape(head_shape)
    value_rows = float_product(normed_input, wv_full).astype(jnp.bfloat16).reshape(head_shape)
    q_scale = rms_scale(query)
    key_scale = rms_scale(key_rows)
    cosine, sine = rope_tables(positions)
    q_rot = rotate(query * q_scale * g_query, cosine, sine).astype(jnp.bfloat16)
    k_rot = rotate(key_rows * key_scale * key_gain, cosine, sine).astype(jnp.bfloat16)
    allowed = (
        (segments[:, :, None] == segments[:, None, :])
        & (positions[:, None, :] <= positions[:, :, None])
    )[:, None]
    scores = (
        jnp.einsum("bqhd,bshd->bhqs", q_rot, k_rot, preferred_element_type=jnp.float32)
        * score_scale
    )
    exponent = jnp.where(allowed, jnp.exp(scores), 0.0)
    denominator = jnp.sum(exponent, axis=-1, keepdims=True)
    probs = exponent / denominator
    probs_round = probs.astype(jnp.bfloat16)
    attended = (
        jnp.einsum("bhqs,bshd->bqhd", probs_round, value_rows, preferred_element_type=jnp.float32)
        .astype(jnp.bfloat16)
    )
    attended_rows = attended.reshape(-1, heads * HEAD_DIM)
    x_rows = tokens.reshape(-1, model_width).astype(jnp.float32)
    mixed_in = x_rows + scatter_ctx(float_product(attended_rows, wo_full), sequence_count)
    scale_mid = rms_scale(mixed_in)
    local_shape = tokens.shape
    normed_mid = gather_ctx(
        (mixed_in * scale_mid * g_mlp).astype(jnp.bfloat16).reshape(local_shape)
    ).reshape(-1, model_width)

    d_hidden = against_rows(grad_all, wd_full)
    gate_up = float_product(normed_mid, gu_full).reshape(-1, shard_size, 2 * ff_width)
    gate_pre = gate_up[:, :, :ff_width].reshape(-1, shard_size * ff_width)
    up_pre = gate_up[:, :, ff_width:].reshape(-1, shard_size * ff_width)
    sigmoid_gate = jax.nn.sigmoid(gate_pre)
    hidden = (gate_pre * sigmoid_gate * up_pre).astype(jnp.bfloat16)
    d_gate = (d_hidden * up_pre * sigmoid_gate * (1.0 + gate_pre * (1.0 - sigmoid_gate))).astype(
        jnp.bfloat16
    )
    d_up = (d_hidden * gate_pre * sigmoid_gate).astype(jnp.bfloat16)
    d_gu = jnp.concatenate(
        [
            d_gate.reshape(-1, shard_size, ff_width),
            d_up.reshape(-1, shard_size, ff_width),
        ],
        axis=2,
    ).reshape(-1, 2 * shard_size * ff_width)
    d_mid = scatter_ctx(against_rows(d_gu, gu_full), sequence_count)
    grad_rows = cotangent.reshape(-1, model_width)
    dg_mlp = jnp.sum(d_mid * mixed_in * scale_mid, axis=0)
    d_resid = grad_rows.astype(jnp.float32) + norm_backward(d_mid, mixed_in, scale_mid, g_mlp)
    resid_all = gather_ctx(d_resid.astype(jnp.bfloat16).reshape(local_shape)).reshape(
        -1, model_width
    )

    block_sum = mixed_in + scatter_ctx(float_product(hidden, wd_full), sequence_count)
    block_out = block_sum.astype(jnp.bfloat16).reshape(local_shape)
    grad_gu = over_tokens(normed_mid, d_gu).astype(jnp.bfloat16)
    grad_gu = grad_gu.reshape(model_width, shard_size, 2 * ff_width)
    owned_gu = lax.psum_scatter(
        jnp.transpose(grad_gu, (1, 0, 2)), "shard", scatter_dimension=0, tiled=False
    )
    grad_down = over_tokens(hidden, grad_all).astype(jnp.bfloat16)
    owned_down = lax.psum_scatter(grad_down, "shard", scatter_dimension=0, tiled=True)
    total_gu, total_down = finish(owned_gu), finish(owned_down)

    d_att = against_rows(resid_all, wo_full).astype(jnp.bfloat16).reshape(head_shape)
    grad_output = over_tokens(attended_rows, resid_all).astype(jnp.bfloat16)
    row_delta = jnp.sum(d_att.astype(jnp.float32) * attended.astype(jnp.float32), axis=-1)
    row_delta = jnp.transpose(row_delta, (0, 2, 1))[..., None]
    d_values = jnp.einsum("bhqs,bqhd->bshd", probs_round, d_att, preferred_element_type=jnp.float32)
    d_probs = jnp.einsum("bqhd,bshd->bhqs", d_att, value_rows, preferred_element_type=jnp.float32)
    d_scores = (probs * (d_probs - row_delta)).astype(jnp.bfloat16)
    d_qrot = (
        jnp.einsum("bhqs,bshd->bqhd", d_scores, k_rot, preferred_element_type=jnp.float32)
        * score_scale
    )
    d_krot = (
        jnp.einsum("bhqs,bqhd->bshd", d_scores, q_rot, preferred_element_type=jnp.float32)
        * score_scale
    )
    d_qn = rotate_back(d_qrot, cosine, sine)
    d_kn = rotate_back(d_krot, cosine, sine)
    dg_query = jnp.sum(d_qn * query * q_scale, axis=(0, 1, 2))
    dg_key = jnp.sum(d_kn * key_rows * key_scale, axis=(0, 1, 2))
    d_query = norm_backward(d_qn, query, q_scale, g_query).astype(jnp.bfloat16)
    d_query = d_query.reshape(-1, heads * HEAD_DIM)
    d_key = norm_backward(d_kn, key_rows, key_scale, key_gain)
    d_key_b = d_key.astype(jnp.bfloat16)
    d_value_b = d_values.astype(jnp.bfloat16)
    d_in_part = (
        against_rows(d_query, wq_full)
        + against_rows(d_key_b.reshape(-1, heads * HEAD_DIM), wk_full)
        + against_rows(d_value_b.reshape(-1, heads * HEAD_DIM), wv_full)
    )
    kv_low = jnp.concatenate([d_key_b[..., :half_width], d_value_b[..., :half_width]], axis=-1)
    kv_high = jnp.concatenate([d_key_b[..., half_width:], d_value_b[..., half_width:]], axis=-1)
    kv_own = jnp.where(odd, kv_high, kv_low)
    kv_other = lax.ppermute(jnp.where(odd, kv_low, kv_high), "ctx", partners)
    slots = kv_other.reshape(
        sequence_count, context_size, local_length, heads, 2 * half_width
    )
    kv_other = jnp.where(odd, jnp.roll(slots, 1, axis=1), jnp.roll(slots, -1, axis=1)).reshape(
        kv_own.shape
    )
    kv_rows = (kv_own.astype(jnp.float32) + kv_other.astype(jnp.float32)).astype(jnp.bfloat16)
    kv_rows = kv_rows.reshape(-1, heads * 2 * half_width)
    d_in = scatter_ctx(d_in_part, sequence_count)
    grad_query = over_tokens(normed_input, d_query).astype(jnp.bfloat16)
    grad_kv = over_tokens(normed_input, kv_rows).astype(jnp.bfloat16)
    grad_qkv = jnp.concatenate(
        [
            grad_query.reshape(model_width, shard_size, HEAD_DIM),
            grad_kv.reshape(model_width, shard_size, 2 * half_width),
        ],
        axis=2,
    )
    dg_attn = jnp.sum(d_in_part * x_full * scale_full, axis=0)
    grad_gains = jnp.concatenate([dg_attn, dg_query, dg_key, dg_mlp])
    gain_parts = slot_order(grad_gains.reshape(shard_size, context_size * gain_count), 1)
    gain_sum = gain_parts[0]
    for k in range(1, context_size):
        gain_sum = gain_sum + shifted(gain_parts[k], -k)
    gain_columns = jnp.pad(
        gain_sum.astype(jnp.bfloat16)[:, :, None], ((0, 0), (0, model_width - gain_count), (0, 7))
    )
    owned_output = lax.psum_scatter(grad_output, "shard", scatter_dimension=0, tiled=True)
    owned_qkv = lax.psum_scatter(
        jnp.concatenate([jnp.transpose(grad_qkv, (1, 0, 2)), gain_columns], axis=2),
        "shard",
        scatter_dimension=0,
        tiled=False,
    )
    total_output, total_qkv = finish(owned_output), finish(owned_qkv)
    scale_in = rms_scale(x_rows)
    grad_input = (d_resid + norm_backward(d_in, x_rows, scale_in, g_attn)).reshape(local_shape)
    return (
        block_out,
        grad_input,
        total_qkv[:, :HEAD_DIM],
        total_qkv[:, HEAD_DIM : HEAD_DIM + half_width],
        total_qkv[:, HEAD_DIM + half_width : HEAD_DIM + 2 * half_width],
        total_output,
        total_gu[:, :ff_width],
        total_gu[:, ff_width:],
        total_down,
        total_qkv[:gain_count, HEAD_DIM + 2 * half_width],
    )


def any_body(*arguments):
    w_query, key_weight = arguments[4:6]
    whole_query_head = w_query.shape[1] == HEAD_DIM
    half_key_head = 2 * key_weight.shape[1] == HEAD_DIM
    if whole_query_head and half_key_head and lax.axis_size("ctx") % 2 == 0:
        return head_parallel_body(*arguments)
    return body(*arguments)


def solution(mesh):
    in_specs = (
        P(("rep", "shard"), "ctx", None),
        P(("rep", "shard"), None),
        P(("rep", "shard"), None),
        P(("rep", "shard"), "ctx", None),
        P(None, ("shard", "ctx")),
        P(None, ("shard", "ctx")),
        P(None, ("shard", "ctx")),
        P(("shard", "ctx"), None),
        P(None, ("shard", "ctx")),
        P(None, ("shard", "ctx")),
        P(("shard", "ctx"), None),
        P(("shard", "ctx")),
    )
    out_specs = (
        P(("rep", "shard"), "ctx", None),
        P(("rep", "shard"), "ctx", None),
        P(None, ("shard", "ctx")),
        P(None, ("shard", "ctx")),
        P(None, ("shard", "ctx")),
        P(("shard", "ctx"), None),
        P(None, ("shard", "ctx")),
        P(None, ("shard", "ctx")),
        P(("shard", "ctx"), None),
        P(("shard", "ctx")),
    )
    return jax.shard_map(any_body, mesh=mesh, in_specs=in_specs, out_specs=out_specs, check_vma=False)
```
